256 devices in a mesh: pipe: 8 (over x, y_lo), dp: 32 (over z, y_hi, core).
Axes of the slice: x: 4, y: 4 (y_hi: 2, y_lo: 2; y = y_hi * 2 + y_lo), z: 8, core: 2. Of those that a mesh axis runs over, the one named last changes fastest.
Arguments:
- master: float32 [8, 3, 3, 256, 256], P('pipe', None, None, 'dp'), may hold values from -6 to 6
- grad_acc: float32 [32, 8, 3, 3, 256, 256], P('dp', 'pipe'), may hold values from -6 to 6
- down_act: float32 [8, 32, 16, 32, 256], P('pipe', 'dp'), may hold values from -6 to 6
- down_next: float32 [32, 16, 32, 256], P('dp'), may hold values from -6 to 6
- up_stash: float32 [8, 32, 2, 16, 32, 256], P('pipe', 'dp'), may hold values from -6 to 6
- up_order: int32 [8, 32, 2], P('pipe', 'dp'), may hold values from 0 to 1, each once within a row
- up_grad: float32 [8, 32, 16, 32, 256], P('pipe', 'dp'), may hold values from -6 to 6
- up_next: float32 [32, 16, 32, 256], P('dp'), may hold values from -6 to 6
- ex_table: float32 [64], replicated, may hold values from 0.25 to 4
- ex_index: int32 [32], P('dp'), may hold values from 0 to 63
Outputs:
- down_out: float32 [8, 32, 16, 32, 256], P('pipe', 'dp')
- up_out: float32 [8, 32, 16, 32, 256], P('pipe', 'dp')
- new_master: float32 [8, 3, 3, 256, 256], P('pipe', None, None, 'dp')
The draws below stay inside these ranges and needn't reach their ends.
Inputs may be any that keep to these rules, and one draw needn't show every extreme that they name: `up_order`: the two entries of a row of the last dimension differ.
All inputs are finite; a program needn't handle non-finite values.
Results may differ from the reference program's by a relative error of at most 0.0044.
Values may be sent and summed in bfloat16 or wider, within the bound.
No kernel may reach another device: no remote copies, remote signals or barrier semaphores. Data moves between devices by JAX's collectives and lax.ppermute only.
A program may use at most 128 MiB of HBM per device.

```python
import math
import jax
import jax.numpy as jnp
from jax import lax

C = 256
HT = 16
WD = 32
TABLE = 64
SECTIONS = 8
EXAMPLES = 32


def place_ends(array, key, least, top_value):
    longest = array.shape.index(max(array.shape))
    spots = []
    for shift in (0, 1):
        where = [jax.random.randint(jax.random.fold_in(key, axis), (), 0, length) for axis, length in enumerate(array.shape)]
        where[longest] = (where[longest] + shift) % array.shape[longest]
        spots.append(tuple(where))
    return array.at[spots[0]].set(least).at[spots[1]].set(top_value)


def with_spikes(values, own_key, source, target, blocks, factor):
    owner, partner = [(jnp.arange(values.shape[axis_at]) // (values.shape[axis_at] // blocks)).reshape([-1 if axis == axis_at else 1 for axis in range(values.ndim)]) for axis_at in (source, target)]
    chosen = jax.random.permutation(own_key, blocks)[partner]
    strong = (owner == chosen) | (owner == (partner + blocks // 2) % blocks)
    return jnp.where(strong, factor * values, values)


def shard_levels(own_key, dims, pieces, smallest, top_value):
    def one(axis_at, blocks):
        steps = jax.random.uniform(jax.random.fold_in(jax.random.fold_in(own_key, 6), axis_at), (blocks,), jnp.float32, smallest / len(pieces), top_value / len(pieces))
        return jnp.repeat(jnp.exp(steps), dims[axis_at] // blocks).reshape((-1,) + (1,) * (len(dims) - axis_at - 1))

    gain = one(*pieces[0])
    for cut in pieces[1:]:
        gain = gain * one(*cut)
    return gain


def centred(rng, shape, spread, reach, cuts=(), kind=jnp.bfloat16):
    factor_of = shard_levels(rng, shape, cuts, -0.22, 0.18) if cuts else 1.0
    drawn = jax.random.normal(rng, shape, jnp.float32) * spread * factor_of
    return jnp.minimum(jnp.maximum(drawn, -reach), reach).astype(kind)


def gaussian_with(stream_key, dims, width, bound, shards, heavy, dtype=jnp.bfloat16):
    array = width * jax.random.normal(stream_key, dims, jnp.float32)
    if shards:
        array = array * shard_levels(stream_key, dims, shards, -0.22, 0.18)
    return jnp.clip(with_spikes(array, jax.random.fold_in(stream_key, 3), *heavy), -bound, bound).astype(dtype)


def setup_inputs(seed: int = 0) -> dict:
    seeds = jax.random.split(jax.random.key(seed), 11)
    master = centred(seeds[0], (SECTIONS, 3, 3, C, C), 1.0, 6.0, ((0, 8), (3, 32)), jnp.float32)
    grad_acc = gaussian_with(seeds[1], (EXAMPLES, SECTIONS, 3, 3, C, C), 1.0, 6.0, ((0, 32), (1, 8)), (0, 4, 32, 2.75), jnp.float32)
    down_act = centred(seeds[2], (SECTIONS, EXAMPLES, HT, WD, C), 1.0, 6.0, ((0, 8), (1, 32)), jnp.float32)
    down_next = centred(seeds[3], (EXAMPLES, HT, WD, C), 1.0, 6.0, ((0, 32),), jnp.float32)
    up_stash = centred(seeds[4], (SECTIONS, EXAMPLES, 2, HT, WD, C), 1.0, 6.0, ((0, 8), (1, 32)), jnp.float32)
    up_order = jax.vmap(lambda own: jax.random.permutation(own, 2))(jax.random.split(seeds[5], SECTIONS * EXAMPLES)).reshape((SECTIONS, EXAMPLES, 2)).astype(jnp.int32)
    up_grad = centred(seeds[6], (SECTIONS, EXAMPLES, HT, WD, C), 1.0, 6.0, ((0, 8), (1, 32)), jnp.float32)
    up_next = centred(seeds[7], (EXAMPLES, HT, WD, C), 1.0, 6.0, ((0, 32),), jnp.float32)
    ex_table = jnp.clip(jnp.exp(jax.random.uniform(seeds[8], (TABLE,), jnp.float32, math.log(0.25), math.log(4.0))), 0.25, 4.0)
    ex_index = place_ends(jax.random.randint(seeds[9], (EXAMPLES,), 0, TABLE), jax.random.fold_in(seeds[9], 1), 0, TABLE - 1).astype(jnp.int32)
    return dict(master=master, grad_acc=grad_acc, down_act=down_act, down_next=down_next, up_stash=up_stash, up_order=up_order, up_grad=up_grad, up_next=up_next, ex_table=ex_table, ex_index=ex_index)


learning_rate = 0.05

def convolve(inputs, kernel):
    return lax.conv_general_dilated(inputs, kernel, (1, 1), 'SAME', dimension_numbers=('NHWC', 'HWIO', 'NHWC'), preferred_element_type=jnp.float32)

def kernel_grad(inputs, delta_bf):
    padded = jnp.pad(inputs, ((0, 0), (1, 1), (1, 1), (0, 0)))
    tile_height = delta_bf.shape[1]
    tile_width = delta_bf.shape[2]
    channels = delta_bf.shape[3]
    flat_delta = delta_bf.reshape(-1, channels)
    grad_rows = []
    for offset_y in range(3):
        grad_cols = []
        for offset_x in range(3):
            window = padded[:, offset_y:offset_y + tile_height, offset_x:offset_x + tile_width, :].reshape(-1, inputs.shape[3])
            grad_cols.append(lax.dot_general(window, flat_delta, (((0,), (0,)), ((), ())), preferred_element_type=jnp.float32))
        grad_rows.append(jnp.stack(grad_cols))
    return jnp.stack(grad_rows)

def section_forward(activation, kernel):
    conv_scale = (9.0 * kernel.shape[2]) ** (-0.5)
    preact = convolve(activation.astype(jnp.bfloat16), kernel) * conv_scale
    return activation + preact * jax.nn.sigmoid(preact)

def section_backward(activation, cotangent, kernel):
    conv_scale = (9.0 * kernel.shape[2]) ** (-0.5)
    inputs = activation.astype(jnp.bfloat16)
    preact = convolve(inputs, kernel) * conv_scale
    sigmoid_value = jax.nn.sigmoid(preact)
    delta_bf = (cotangent * sigmoid_value * (1.0 + preact * (1.0 - sigmoid_value))).astype(jnp.bfloat16)
    flipped = jnp.transpose(kernel[::-1, ::-1], (0, 1, 3, 2))
    back_field = cotangent + convolve(delta_bf, flipped) * conv_scale
    kernel_grads = kernel_grad(inputs, delta_bf) * conv_scale
    return (back_field, kernel_grads)

def run_forward(operands):
    return section_forward(operands[0], operands[1])

def run_backward(operands):
    return section_backward(operands[0], operands[1], operands[2])

def reference(master, grad_acc, down_act, down_next, up_stash, up_order, up_grad, up_next, ex_table, ex_index):
    weights = master.astype(jnp.bfloat16)
    mirror = weights[::-1]
    section_out = lax.map(run_forward, (down_act, weights))
    inflow = jnp.concatenate([down_next[None], section_out[:-1]], axis=0)
    down_out = lax.map(run_forward, (inflow, weights))
    slot_zero = up_stash[:, :, 0]
    slot_one = up_stash[:, :, 1]
    first_input = jnp.where((up_order[:, :, 0] == 0)[:, :, None, None, None], slot_zero, slot_one)
    second_input = jnp.where((up_order[:, :, 1] == 0)[:, :, None, None, None], slot_zero, slot_one)
    back_first, grad_first = lax.map(run_backward, (first_input, up_grad, mirror))
    entering = up_next * ex_table[ex_index][:, None, None, None]
    cot_second = jnp.concatenate([entering[None], back_first[:-1]], axis=0)
    up_out, grad_second = lax.map(run_backward, (second_input, cot_second, mirror))
    up_grads = grad_first + grad_second
    total_grad = lax.optimization_barrier(jnp.sum(grad_acc, axis=0)) + up_grads[::-1]
    new_master = master - learning_rate * total_grad
    return (down_out, up_out, new_master)
```

```python
import functools

import jax
import jax.numpy as jnp
from jax import lax
from jax.experimental import pallas as pl
from jax.experimental.pallas import tpu as pltpu
from jax.sharding import PartitionSpec as P


learning_rate = 0.05
PIPE, Z, Y, CORES = 8, 8, 2, 2
C, HT, WD = 256, 16, 32
PIX = HT * WD
PADDED = PIX + 2 * WD
TAPS = 9
SCALE = (9.0 * C) ** (-0.5)
bf16, f32 = jnp.bfloat16, jnp.float32
VM = pl.BlockSpec(memory_space=pltpu.VMEM)
SM = pl.BlockSpec(memory_space=pltpu.SMEM)


def moved(value, where):
    pairs = []
    for p in range(PIPE):
        for z in range(Z):
            for y in range(Y):
                for c in range(CORES):
                    to = where(p, z, y, c)
                    if to is None:
                        continue
                    tp, tz, ty, tc = to
                    if not 0 <= tp < PIPE:
                        continue
                    target = tp * 32 + (tz % Z) * 4 + ty * 2 + tc
                    pairs.append((p * 32 + z * 4 + y * 2 + c, target))
    return lax.ppermute(value, ("pipe", "dp"), pairs)


def to_core(value):
    return moved(value, lambda p, z, y, c: (p, z, y, 1 - c))


def to_y(value):
    return moved(value, lambda p, z, y, c: (p, z, 1 - y, c))


def to_mirror(value):
    return moved(value, lambda p, z, y, c: (PIPE - 1 - p, z, y, c))


def to_mirror_y(value):
    return moved(value, lambda p, z, y, c: (PIPE - 1 - p, z, 1 - y, c))


def to_next(value):
    return moved(value, lambda p, z, y, c: (p + 1, z, y, c))


def place():
    dp = lax.axis_index("dp")
    return dp // 4, (dp // 2) % 2, dp % 2


def call(kernel, outs, args, specs=None, scratch=(), flops=0):
    size = sum(a.size * a.dtype.itemsize for a in args) + sum(
        int(o.size) * o.dtype.itemsize for o in outs
    )
    result = pl.pallas_call(
        kernel,
        out_shape=outs,
        in_specs=specs or [VM] * len(args),
        out_specs=[VM] * len(outs),
        scratch_shapes=list(scratch),
        compiler_params=pltpu.CompilerParams(vmem_limit_bytes=40 << 20),
        cost_estimate=pl.CostEstimate(flops=flops, bytes_accessed=size, transcendentals=0),
    )(*args)
    return result


def shape(dims, dtype):
    return jax.ShapeDtypeStruct(dims, dtype)


def three_shifts(u):
    column = lax.broadcasted_iota(jnp.int32, u.shape, 0) % WD
    left = jnp.where(column == 0, 0.0, pltpu.roll(u, 1, 0))
    right = jnp.where(column == WD - 1, 0.0, pltpu.roll(u, PIX - 1, 0))
    return jnp.concatenate([left.astype(bf16), u.astype(bf16), right.astype(bf16)], axis=1)


def fill_padded(ref, value):
    edge = jnp.zeros((WD, value.shape[1]), value.dtype)
    ref[pl.ds(0, WD), :] = edge
    ref[pl.ds(WD, PIX), :] = value
    ref[pl.ds(WD + PIX, WD), :] = edge


def conv(col_ref, w_ref):
    total = None
    for a in range(3):
        part = jnp.dot(
            col_ref[pl.ds(a * WD, PIX), :],
            w_ref[pl.ds(3 * a, 3)].reshape(3 * C, C),
            preferred_element_type=f32,
        )
        total = part if total is None else total + part
    return total * SCALE


def conv_back(col_ref, w_ref):
    total = None
    for a in range(3):
        for b in range(3):
            part = lax.dot_general(
                col_ref[pl.ds((2 - a) * WD, PIX), pl.ds((2 - b) * C, C)],
                w_ref[3 * a + b],
                (((1,), (1,)), ((), ())),
                preferred_element_type=f32,
            )
            total = part if total is None else total + part
    return total * SCALE


def grads(xt_ref, dpad_ref, store):
    for a in range(3):
        g = jnp.dot(
            xt_ref[...], dpad_ref[pl.ds((2 - a) * WD, PIX), :], preferred_element_type=f32
        )
        for b in range(3):
            store(3 * a + b, (g[b * C : (b + 1) * C] * SCALE).reshape(Z, Y, 16, C))


def assemble_kernel(a_ref, b_ref, c_ref, d_ref, w_ref):
    z, y, core = place()
    for ref, same_core, same_y in (
        (a_ref, True, True),
        (b_ref, True, False),
        (c_ref, False, True),
        (d_ref, False, False),
    ):
        kind = core if same_core else 1 - core
        half = y if same_y else 1 - y
        for s in range(4):
            low = (z + (7 - s if s < 3 else 0)) % Z
            high = (z + 1 + s) % Z
            source = jnp.where(kind == 0, low, high)
            w_ref[:, source * 2 + half] = ref[s]


def prep_kernel(u_ref, col_ref):
    fill_padded(col_ref, three_shifts(u_ref[...]))


def prep_stash_kernel(order_ref, stash_ref, col1_ref, xt1_ref, col2_ref, xt2_ref):
    for slot, col_ref, xt_ref in ((0, col1_ref, xt1_ref), (1, col2_ref, xt2_ref)):
        v3 = three_shifts(stash_ref[order_ref[0, slot]])
        fill_padded(col_ref, v3)
        xt_ref[...] = v3.T


def forward_first_kernel(col_ref, u_ref, w_ref, out_ref):
    pre = conv(col_ref, w_ref)
    out_ref[...] = (u_ref[...] + pre * jax.nn.sigmoid(pre)).astype(bf16)


def forward_second_kernel(arrived_ref, next_ref, w_ref, out_ref, col_ref):
    first = lax.axis_index("pipe") == 0
    u = jnp.where(first, next_ref[...], arrived_ref[...].astype(f32))
    fill_padded(col_ref, three_shifts(u))
    pre = conv(col_ref, w_ref)
    out_ref[...] = u + pre * jax.nn.sigmoid(pre)


def up_first_kernel(col_ref, g_ref, w_ref, back_ref, dpad_ref, dcol_ref):
    pre = conv(col_ref, w_ref)
    s = jax.nn.sigmoid(pre)
    g = g_ref[...]
    delta = (g * s * (1.0 + pre * (1.0 - s))).astype(bf16)
    fill_padded(dpad_ref, delta)
    fill_padded(dcol_ref, three_shifts(delta.astype(f32)))
    back_ref[...] = (g + conv_back(dcol_ref, w_ref)).astype(bf16)


def slope_kernel(col_ref, w_ref, slope_ref):
    pre = conv(col_ref, w_ref)
    s = jax.nn.sigmoid(pre)
    slope_ref[...] = s * (1.0 + pre * (1.0 - s))


def grad_first_kernel(xt_ref, dpad_ref, g_ref):
    def store(tap, value):
        g_ref[tap] = value

    grads(xt_ref, dpad_ref, store)


def share_out(total_ref, keep_ref, send_ref):
    z, _, core = place()
    for j in range(4):
        mine = (z + 4 * core + j) % Z
        theirs = (z + 4 * core + 4 + j) % Z
        for tap in range(TAPS):
            keep_ref[j, :, tap] = total_ref[tap, mine]
            send_ref[j, :, tap] = total_ref[tap, theirs].astype(bf16)


def up_second_kernel(
    table_ref, index_ref, arrived_ref, next_ref, slope_ref, xt_ref, g_ref,
    keep_ref, send_ref, dpad_ref, cot_ref, total_ref,
):
    first = lax.axis_index("pipe") == 0
    factor = table_ref[index_ref[0]]
    cot = jnp.where(first, next_ref[...] * factor, arrived_ref[...].astype(f32))
    cot_ref[...] = cot
    fill_padded(dpad_ref, (cot * slope_ref[...]).astype(bf16))

    def store(tap, value):
        total_ref[tap] = g_ref[tap] + value

    grads(xt_ref, dpad_ref, store)
    share_out(total_ref, keep_ref, send_ref)


def up_out_kernel(cot_ref, dpad_ref, w_ref, out_ref, dcol_ref):
    delta = dpad_ref[pl.ds(WD, PIX), :].astype(f32)
    fill_padded(dcol_ref, three_shifts(delta))
    out_ref[...] = cot_ref[...] + conv_back(dcol_ref, w_ref)


def earlier_kernel(acc_ref, keep_ref, send_ref):
    share_out(acc_ref, keep_ref, send_ref)


def core_sum_kernel(keep_ref, got_ref, mine_ref, send_ref):
    _, y, _ = place()
    for j in range(4):
        mine_ref[j] = keep_ref[j, y] + got_ref[j, y].astype(f32)
        send_ref[j] = (keep_ref[j, 1 - y] + got_ref[j, 1 - y].astype(f32)).astype(bf16)


def earlier_sum_kernel(mine_ref, got_ref, out_ref):
    out_ref[...] = (mine_ref[...] + got_ref[...].astype(f32)).astype(bf16)


def y_sum_kernel(mine_ref, got_ref, earlier_ref, *out_refs):
    for j in range(4):
        total = mine_ref[j] + got_ref[j].astype(f32) + earlier_ref[j].astype(f32)
        out_refs[j][...] = total.astype(bf16)


def z_sum_kernel(m0_ref, m1_ref, m2_ref, m3_ref, mine_ref, send_ref, total_ref):
    _, _, core = place()
    total = (m0_ref[...].astype(f32) + m1_ref[...].astype(f32)) + (
        m2_ref[...].astype(f32) + m3_ref[...].astype(f32)
    )
    total_ref[...] = total.reshape(TAPS, CORES, 8, C)
    mine_ref[...] = total_ref[:, core]
    send_ref[...] = total_ref[:, 1 - core].astype(bf16)


CONV_FLOPS = 2 * PIX * TAPS * C * C
COL = shape((PADDED, 3 * C), bf16)
DPAD = shape((PADDED, C), bf16)
FIELD = shape((PIX, C), f32)
FIELD16 = shape((PIX, C), bf16)
COL_SCRATCH = pltpu.VMEM((PADDED, 3 * C), bf16)
TOTAL = shape((TAPS, Z, Y, 16, C), f32)


def gather_weights(own, core):
    other = to_core(own)
    low = jnp.where(core == 0, own, other)
    high = jnp.where(core == 0, other, own)
    chunk = jnp.concatenate([low, high], axis=1)
    got = [
        moved(chunk, lambda p, z, y, c, k=k: (p, z + k if c == 0 else z - k, y, c))
        for k in (1, 2, 3)
    ]
    far = moved(chunk, lambda p, z, y, c: (p, z - 4, y, c) if c == 1 else None)
    payload = jnp.stack(got + [jnp.where(core == 0, chunk, far)])
    mirror_same = to_mirror(payload)
    mirror_other = to_mirror_y(payload)
    own_other = to_y(payload)

    def assembled(same, other_y):
        w = call(
            assemble_kernel,
            [shape((TAPS, 16, 16, C), bf16)],
            [same, other_y, to_core(same), to_core(other_y)],
        )[0]
        return w.reshape(TAPS, C, C)

    return assembled(payload, own_other), assembled(mirror_same, mirror_other)


def body(
    master, grad_acc, down_act, down_next, up_stash, up_order, up_grad, up_next, ex_table, ex_index
):
    core = lax.axis_index("dp") % 2
    own = master.reshape(TAPS, 8, C).astype(bf16)
    w_own, w_mirror = gather_weights(own, core)

    act = down_act.reshape(PIX, C)
    stash = up_stash.reshape(2, PIX, C)
    col1, xt1, col2, xt2 = call(
        prep_stash_kernel,
        [COL, shape((3 * C, PIX), bf16)] * 2,
        [up_order[0], stash],
        [SM, VM],
    )
    col_down = call(prep_kernel, [COL], [act])[0]

    halves = [shape((4, Y, TAPS, 16, C), f32), shape((4, Y, TAPS, 16, C), bf16)]
    quarters = [shape((4, TAPS, 16, C), f32), shape((4, TAPS, 16, C), bf16)]
    keep_e, send_e = call(earlier_kernel, halves, [grad_acc.reshape(TAPS, Z, Y, 16, C)])
    mine_e, over_e = call(core_sum_kernel, quarters, [keep_e, to_core(send_e)])
    earlier = call(earlier_sum_kernel, quarters[1:], [mine_e, to_y(over_e)])[0]
    earlier = to_mirror(earlier)

    back, dpad1 = call(
        up_first_kernel,
        [FIELD16, DPAD],
        [col1, up_grad.reshape(PIX, C), w_mirror],
        scratch=[COL_SCRATCH],
        flops=2 * CONV_FLOPS,
    )
    passed = to_next(back)
    slope = call(slope_kernel, [FIELD], [col2, w_mirror], flops=CONV_FLOPS)[0]
    g1 = call(grad_first_kernel, [TOTAL], [xt1, dpad1], flops=CONV_FLOPS)[0]

    section_out = call(
        forward_first_kernel, [FIELD16], [col_down, act, w_own], flops=CONV_FLOPS
    )[0]
    arrived = to_next(section_out)
    down_out = call(
        forward_second_kernel,
        [FIELD],
        [arrived, down_next.reshape(PIX, C), w_own],
        scratch=[COL_SCRATCH],
        flops=CONV_FLOPS,
    )[0]

    keep, send, dpad2, cot = call(
        up_second_kernel,
        halves + [DPAD, FIELD],
        [ex_table, ex_index, passed, up_next.reshape(PIX, C), slope, xt2, g1],
        [SM, SM, VM, VM, VM, VM, VM],
        scratch=[pltpu.VMEM((TAPS, Z, Y, 16, C), f32)],
        flops=CONV_FLOPS,
    )
    up_out = call(
        up_out_kernel, [FIELD], [cot, dpad2, w_mirror], scratch=[COL_SCRATCH], flops=CONV_FLOPS
    )[0]

    mine, over = call(core_sum_kernel, quarters, [keep, to_core(send)])
    messages = call(
        y_sum_kernel, [shape((TAPS, 16, C), bf16)] * 4, [mine, to_y(over), earlier]
    )
    got = [
        moved(m, lambda p, z, y, c, j=j: (PIPE - 1 - p, z + 4 * c + j, y, c))
        for j, m in enumerate(messages)
    ]
    mine, last = call(
        z_sum_kernel,
        [shape((TAPS, 8, C), f32), shape((TAPS, 8, C), bf16)],
        got,
        scratch=[pltpu.VMEM((TAPS, CORES, 8, C), f32)],
    )
    total_grad = mine + to_core(last).astype(f32)
    new_master = master - learning_rate * total_grad.reshape(master.shape)
    field = (1, 1, HT, WD, C)
    return (down_out.reshape(field), up_out.reshape(field), new_master)


def solution(mesh):
    return jax.shard_map(
        body,
        mesh=mesh,
        in_specs=(
            P("pipe", None, None, "dp", None),
            P("dp", "pipe", None, None, None, None),
            P("pipe", "dp", None, None, None),
            P("dp", None, None, None),
            P("pipe", "dp", None, None, None, None),
            P("pipe", "dp", None),
            P("pipe", "dp", None, None, None),
            P("dp", None, None, None),
            P(),
            P("dp"),
        ),
        out_specs=(
            P("pipe", "dp", None, None, None),
            P("pipe", "dp", None, None, None),
            P("pipe", None, None, "dp", None),
        ),
        check_vma=False,
    )
```

```python
import jax
import jax.numpy as jnp
from jax import lax
from jax.experimental import pallas as pl
from jax.experimental.pallas import tpu as pltpu
from jax.sharding import PartitionSpec as P


learning_rate = 0.05
PIPE, Z, Y, CORES = 8, 8, 2, 2
C, HT, WD = 256, 16, 32
PIX = HT * WD
PADDED = PIX + 2 * WD
TAPS = 9
SCALE = (9.0 * C) ** (-0.5)
bf16, f32 = jnp.bfloat16, jnp.float32
VM = pl.BlockSpec(memory_space=pltpu.VMEM)
SM = pl.BlockSpec(memory_space=pltpu.SMEM)


def moved(value, where):
    pairs = []
    for p in range(PIPE):
        for z in range(Z):
            for y in range(Y):
                for c in range(CORES):
                    to = where(p, z, y, c)
                    if to is None:
                        continue
                    tp, tz, ty, tc = to
                    if not 0 <= tp < PIPE:
                        continue
                    target = tp * 32 + (tz % Z) * 4 + ty * 2 + tc
                    pairs.append((p * 32 + z * 4 + y * 2 + c, target))
    return lax.ppermute(value, ("pipe", "dp"), pairs)


def to_core(value):
    return moved(value, lambda p, z, y, c: (p, z, y, 1 - c))


def to_y(value):
    return moved(value, lambda p, z, y, c: (p, z, 1 - y, c))


def to_mirror(value):
    return moved(value, lambda p, z, y, c: (PIPE - 1 - p, z, y, c))


def to_plane(value, flip, far):
    def where(p, z, y, c):
        return (PIPE - 1 - p if flip else p, z + 4 * far, y ^ c, c)

    return moved(value, where)


def to_owner(value, far):
    return moved(value, lambda p, z, y, c: (PIPE - 1 - p, z + 4 * (c ^ far), c, y))


def to_next(value):
    return moved(value, lambda p, z, y, c: (p + 1, z, y, c))


def to_z(value, k):
    return moved(value, lambda p, z, y, c: (p, z + k if c == 0 else z - k, y, c))


def place():
    dp = lax.axis_index("dp")
    return dp // 4, (dp // 2) % 2, dp % 2


def call(kernel, outs, args, specs=None, scratch=(), flops=0, after=()):
    specs = specs or [VM] * len(args)
    if after:
        used, body = len(args), kernel

        def kernel(*refs):
            body(*refs[:used], *refs[used + len(after) :])

    size = sum(a.size * a.dtype.itemsize for a in args) + sum(
        int(o.size) * o.dtype.itemsize for o in outs
    )
    return pl.pallas_call(
        kernel,
        out_shape=outs,
        in_specs=specs + [pl.BlockSpec(memory_space=pl.ANY)] * len(after),
        out_specs=[VM] * len(outs),
        scratch_shapes=list(scratch),
        compiler_params=pltpu.CompilerParams(vmem_limit_bytes=40 << 20),
        cost_estimate=pl.CostEstimate(flops=flops, bytes_accessed=size, transcendentals=0),
    )(*args, *after)


def shape(dims, dtype):
    return jax.ShapeDtypeStruct(dims, dtype)


def three_shifts(u):
    column = lax.broadcasted_iota(jnp.int32, u.shape, 0) % WD
    left = jnp.where(column == 0, 0.0, pltpu.roll(u, 1, 0))
    right = jnp.where(column == WD - 1, 0.0, pltpu.roll(u, PIX - 1, 0))
    return jnp.concatenate([left.astype(bf16), u.astype(bf16), right.astype(bf16)], axis=1)


def fill_padded(ref, value):
    edge = jnp.zeros((WD, value.shape[1]), value.dtype)
    ref[pl.ds(0, WD), :] = edge
    ref[pl.ds(WD, PIX), :] = value
    ref[pl.ds(WD + PIX, WD), :] = edge


def conv(col_ref, w_ref):
    total = None
    for a in range(3):
        part = jnp.dot(
            col_ref[pl.ds(a * WD, PIX), :],
            w_ref[pl.ds(3 * a, 3)].reshape(3 * C, C),
            preferred_element_type=f32,
        )
        total = part if total is None else total + part
    return total * SCALE


def conv_back(col_ref, w_ref):
    total = None
    for a in range(3):
        for b in range(3):
            part = lax.dot_general(
                col_ref[pl.ds((2 - a) * WD, PIX), pl.ds((2 - b) * C, C)],
                w_ref[3 * a + b],
                (((1,), (1,)), ((), ())),
                preferred_element_type=f32,
            )
            total = part if total is None else total + part
    return total * SCALE


def grads(xt_ref, dpad_ref, store):
    for a in range(3):
        g = jnp.dot(
            xt_ref[...], dpad_ref[pl.ds((2 - a) * WD, PIX), :], preferred_element_type=f32
        )
        for b in range(3):
            store(3 * a + b, (g[b * C : (b + 1) * C] * SCALE).reshape(Z * Y, 16, C))


def pair_kernel(own_ref, other_ref, pair_ref):
    _, _, core = place()
    mine, theirs = own_ref[...].astype(f32), other_ref[...].astype(f32)
    low, high = jnp.where(core == 0, mine, theirs), jnp.where(core == 0, theirs, mine)
    pair_ref[...] = jnp.concatenate([low, high], axis=1).astype(bf16)


def fill_plane(chunk_ref, half_ref, near, far):
    _, y, core = place()
    half = y ^ core
    chunk_ref[0, near[0]] = near[1][...]
    chunk_ref[0, 1 - near[0]] = near[2][...]
    chunk_ref[1, half] = far[0][...]
    chunk_ref[1, 1 - half] = far[1][...]
    for dz in range(2):
        half_ref[dz] = chunk_ref[dz, core]


def plane_mirror_kernel(near_ref, near_core_ref, far_ref, far_core_ref, chunk_ref, half_ref):
    _, y, core = place()
    fill_plane(chunk_ref, half_ref, (y ^ core, near_ref, near_core_ref), (far_ref, far_core_ref))


def plane_own_kernel(pair_ref, other_ref, far_ref, far_core_ref, chunk_ref, half_ref):
    _, y, _ = place()
    fill_plane(chunk_ref, half_ref, (y, pair_ref, other_ref), (far_ref, far_core_ref))


def assemble_kernel(chunk_ref, one_ref, one_core_ref, two_ref, two_core_ref, w_ref):
    z, _, core = place()
    sign = 2 * core - 1

    def put(source_z, source_y, value):
        w_ref[:, lax.rem(source_z + 2 * Z, Z) * 2 + source_y] = value

    for dz in range(2):
        for half in range(Y):
            put(z + 4 * dz, half, chunk_ref[dz, half])
            put(z + sign + 4 * dz, half, one_ref[dz, half])
            put(z - sign + 4 * dz, half, one_core_ref[dz, half])
        put(z + 2 * sign + 4 * dz, core, two_ref[dz])
        put(z - 2 * sign + 4 * dz, 1 - core, two_core_ref[dz])


def prep_kernel(u_ref, col_ref):
    fill_padded(col_ref, three_shifts(u_ref[...]))


def prep_stash_kernel(order_ref, stash_ref, col1_ref, xt1_ref, col2_ref, xt2_ref):
    for slot, col_ref, xt_ref in ((0, col1_ref, xt1_ref), (1, col2_ref, xt2_ref)):
        v3 = three_shifts(stash_ref[order_ref[0, slot]])
        fill_padded(col_ref, v3)
        xt_ref[...] = v3.T


def forward_first_kernel(col_ref, u_ref, w_ref, out_ref):
    pre = conv(col_ref, w_ref)
    out_ref[...] = (u_ref[...] + pre * jax.nn.sigmoid(pre)).astype(bf16)


def forward_second_kernel(arrived_ref, next_ref, w_ref, out_ref, col_ref):
    first = lax.axis_index("pipe") == 0
    u = jnp.where(first, next_ref[...], arrived_ref[...].astype(f32))
    fill_padded(col_ref, three_shifts(u))
    pre = conv(col_ref, w_ref)
    out_ref[...] = u + pre * jax.nn.sigmoid(pre)


def up_first_kernel(col_ref, g_ref, w_ref, back_ref, dpad_ref, dcol_ref):
    pre = conv(col_ref, w_ref)
    s = jax.nn.sigmoid(pre)
    g = g_ref[...]
    delta = (g * s * (1.0 + pre * (1.0 - s))).astype(bf16)
    fill_padded(dpad_ref, delta)
    fill_padded(dcol_ref, three_shifts(delta.astype(f32)))
    back_ref[...] = (g + conv_back(dcol_ref, w_ref)).astype(bf16)


def slope_kernel(col_ref, w_ref, slope_ref):
    pre = conv(col_ref, w_ref)
    s = jax.nn.sigmoid(pre)
    slope_ref[...] = s * (1.0 + pre * (1.0 - s))


def grad_first_kernel(xt_ref, dpad_ref, g_ref):
    def store(tap, value):
        g_ref[tap] = value

    grads(xt_ref, dpad_ref, store)


def share_out(total_ref, keep_ref, send_ref):
    z, _, core = place()
    sign = 1 - 2 * core

    def put(j, mine, theirs, mine_y, theirs_y):
        keep_ref[j] = total_ref[:, lax.rem(mine + 2 * Z, Z) * 2 + mine_y]
        send_ref[j] = total_ref[:, lax.rem(theirs + 2 * Z, Z) * 2 + theirs_y].astype(bf16)

    for dz in range(2):
        at = z + 4 * dz
        for half in range(Y):
            put(2 * dz + half, at + sign, at - sign, half, half)
        put(4 + dz, at + 2 * sign, at - 2 * sign, core, 1 - core)
        put(6 + dz, at, at, core, 1 - core)


def up_second_kernel(
    table_ref, index_ref, arrived_ref, next_ref, slope_ref, xt_ref, g_ref,
    keep_ref, send_ref, dpad_ref, cot_ref, total_ref,
):
    first = lax.axis_index("pipe") == 0
    factor = table_ref[index_ref[0]]
    cot = jnp.where(first, next_ref[...] * factor, arrived_ref[...].astype(f32))
    cot_ref[...] = cot
    fill_padded(dpad_ref, (cot * slope_ref[...]).astype(bf16))

    def store(tap, value):
        total_ref[tap] = g_ref[tap] + value

    grads(xt_ref, dpad_ref, store)
    share_out(total_ref, keep_ref, send_ref)


def up_out_kernel(cot_ref, dpad_ref, w_ref, out_ref, dcol_ref):
    delta = dpad_ref[pl.ds(WD, PIX), :].astype(f32)
    fill_padded(dcol_ref, three_shifts(delta))
    out_ref[...] = cot_ref[...] + conv_back(dcol_ref, w_ref)


def earlier_kernel(acc_ref, keep_ref, send_ref):
    share_out(acc_ref, keep_ref, send_ref)


def earlier_sum_kernel(keep_ref, got_ref, out_ref):
    out_ref[...] = (keep_ref[...] + got_ref[...].astype(f32)).astype(bf16)


def core_sum_kernel(keep_ref, got_ref, earlier_ref, one_ref, two_ref, mine_ref):
    def total(j):
        return keep_ref[j] + got_ref[j].astype(f32) + earlier_ref[j].astype(f32)

    for dz in range(2):
        for half in range(Y):
            one_ref[dz, half] = total(2 * dz + half).astype(bf16)
        two_ref[dz] = total(4 + dz).astype(bf16)
        mine_ref[dz] = total(6 + dz)


def z_sum_kernel(one_ref, two_ref, mine_ref, keep_ref, send_ref):
    _, _, core = place()
    for dz in range(2):
        keep_ref[dz] = mine_ref[dz] + two_ref[dz].astype(f32) + one_ref[dz, core].astype(f32)
        send_ref[dz] = one_ref[dz, 1 - core]


def z_core_sum_kernel(keep_ref, got_ref, near_ref, far_ref):
    _, _, core = place()
    for dz, out_ref in ((core, near_ref), (1 - core, far_ref)):
        out_ref[...] = (keep_ref[dz] + got_ref[dz].astype(f32)).astype(bf16)


def last_sum_kernel(a_ref, b_ref, keep_ref, send_ref, total_ref):
    _, _, core = place()
    total = a_ref[...].astype(f32) + b_ref[...].astype(f32)
    total_ref[...] = total.reshape(TAPS, CORES, 8, C)
    keep_ref[...] = total_ref[:, core]
    send_ref[...] = total_ref[:, 1 - core].astype(bf16)


CONV_FLOPS = 2 * PIX * TAPS * C * C
COL = shape((PADDED, 3 * C), bf16)
DPAD = shape((PADDED, C), bf16)
FIELD = shape((PIX, C), f32)
FIELD16 = shape((PIX, C), bf16)
COL_SCRATCH = pltpu.VMEM((PADDED, 3 * C), bf16)
TOTAL = shape((TAPS, Z * Y, 16, C), f32)
CHUNK = shape((2, Y, TAPS, 16, C), bf16)
HALF = shape((2, TAPS, 16, C), bf16)
PAIR = shape((TAPS, 16, C), bf16)


def assembled(chunk, half):
    one, two = to_z(chunk, 1), to_z(half, 2)
    args = [chunk, one, to_core(one), two, to_core(two)]
    w = call(assemble_kernel, [shape((TAPS, 16, 16, C), bf16)], args)[0]
    return w.reshape(TAPS, C, C)


def body(
    master, grad_acc, down_act, down_next, up_stash, up_order, up_grad, up_next, ex_table, ex_index
):
    own = master.reshape(TAPS, 8, C).astype(bf16)
    pair = call(pair_kernel, [PAIR], [own, to_core(own)])[0]

    far = to_plane(pair, True, 1)
    near = to_plane(pair, True, 0)
    chunk, half = call(plane_mirror_kernel, [CHUNK, HALF], [near, to_core(near), far, to_core(far)])
    w_mirror = assembled(chunk, half)

    own_other = to_y(pair)
    own_far = to_plane(pair, False, 1)
    act = down_act.reshape(PIX, C)
    stash = up_stash.reshape(2, PIX, C)
    col1, xt1, col2, xt2 = call(
        prep_stash_kernel, [COL, shape((3 * C, PIX), bf16)] * 2, [up_order[0], stash], [SM, VM]
    )
    col_down = call(prep_kernel, [COL], [act])[0]

    lists = [shape((8, TAPS, 16, C), f32), shape((8, TAPS, 16, C), bf16)]
    keep_e, send_e = call(earlier_kernel, lists, [grad_acc.reshape(TAPS, Z * Y, 16, C)])
    earlier = call(earlier_sum_kernel, lists[1:], [keep_e, to_core(send_e)])[0]
    earlier_moved = to_mirror(earlier)

    back, dpad1 = call(
        up_first_kernel,
        [FIELD16, DPAD],
        [col1, up_grad.reshape(PIX, C), w_mirror],
        scratch=[COL_SCRATCH],
        flops=2 * CONV_FLOPS,
    )
    passed = to_next(back)
    own_chunk, own_half = call(
        plane_own_kernel, [CHUNK, HALF], [pair, own_other, own_far, to_core(own_far)]
    )
    slope = call(slope_kernel, [FIELD], [col2, w_mirror], flops=CONV_FLOPS)[0]
    g1 = call(grad_first_kernel, [TOTAL], [xt1, dpad1], flops=CONV_FLOPS)[0]

    keep, send, dpad2, cot = call(
        up_second_kernel,
        lists + [DPAD, FIELD],
        [ex_table, ex_index, passed, up_next.reshape(PIX, C), slope, xt2, g1],
        [SM, SM, VM, VM, VM, VM, VM],
        scratch=[pltpu.VMEM((TAPS, Z * Y, 16, C), f32)],
        flops=CONV_FLOPS,
    )

    one, two, mine = call(
        core_sum_kernel, [CHUNK, HALF, shape(HALF.shape, f32)], [keep, to_core(send), earlier_moved]
    )
    got = [to_z(one, 1), to_z(two, 2)]

    w_own = assembled(own_chunk, own_half)
    section_out = call(forward_first_kernel, [FIELD16], [col_down, act, w_own], flops=CONV_FLOPS)[0]
    arrived = to_next(section_out)
    up_out = call(
        up_out_kernel, [FIELD], [cot, dpad2, w_mirror], scratch=[COL_SCRATCH], flops=CONV_FLOPS
    )[0]
    down_out = call(
        forward_second_kernel,
        [FIELD],
        [arrived, down_next.reshape(PIX, C), w_own],
        scratch=[COL_SCRATCH],
        flops=CONV_FLOPS,
    )[0]

    keep_z, send_z = call(z_sum_kernel, [shape(HALF.shape, f32), HALF], got + [mine])
    first, second = call(z_core_sum_kernel, [PAIR] * 2, [keep_z, to_core(send_z)])
    keep_l, send_l = call(
        last_sum_kernel,
        [shape((TAPS, 8, C), f32), shape((TAPS, 8, C), bf16)],
        [to_owner(first, 0), to_owner(second, 1)],
        scratch=[pltpu.VMEM((TAPS, CORES, 8, C), f32)],
    )
    got_l = to_core(send_l)
    total_grad = keep_l + got_l.astype(f32)
    new_master = master - learning_rate * total_grad.reshape(master.shape)
    field = (1, 1, HT, WD, C)
    return (down_out.reshape(field), up_out.reshape(field), new_master)


def solution(mesh):
    return jax.shard_map(
        body,
        mesh=mesh,
        in_specs=(
            P("pipe", None, None, "dp", None),
            P("dp", "pipe", None, None, None, None),
            P("pipe", "dp", None, None, None),
            P("dp", None, None, None),
            P("pipe", "dp", None, None, None, None),
            P("pipe", "dp", None),
            P("pipe", "dp", None, None, None),
            P("dp", None, None, None),
            P(),
            P("dp"),
        ),
        out_specs=(
            P("pipe", "dp", None, None, None),
            P("pipe", "dp", None, None, None),
            P("pipe", None, None, "dp", None),
        ),
        check_vma=False,
    )
```

```python
import functools

import jax
import jax.numpy as jnp
from jax import lax
from jax.experimental import pallas as pl
from jax.experimental.pallas import tpu as pltpu
from jax.sharding import PartitionSpec as P


learning_rate = 0.05
PIPE, Z, Y, CORES = 8, 8, 2, 2
C, HT, WD = 256, 16, 32
PIX = HT * WD
PADDED = PIX + 2 * WD
TAPS = 9
SCALE = (9.0 * C) ** (-0.5)
bf16, f32 = jnp.bfloat16, jnp.float32
VM = pl.BlockSpec(memory_space=pltpu.VMEM)
SM = pl.BlockSpec(memory_space=pltpu.SMEM)


def moved(value, where):
    pairs = []
    for p in range(PIPE):
        for z in range(Z):
            for y in range(Y):
                for c in range(CORES):
                    to = where(p, z, y, c)
                    if to is None:
                        continue
                    tp, tz, ty, tc = to
                    if not 0 <= tp < PIPE:
                        continue
                    target = tp * 32 + (tz % Z) * 4 + ty * 2 + tc
                    pairs.append((p * 32 + z * 4 + y * 2 + c, target))
    return lax.ppermute(value, ("pipe", "dp"), pairs)


def to_core(value):
    return moved(value, lambda p, z, y, c: (p, z, y, 1 - c))


def to_y(value):
    return moved(value, lambda p, z, y, c: (p, z, 1 - y, c))


def to_mirror(value):
    return moved(value, lambda p, z, y, c: (PIPE - 1 - p, z, y, c))


def to_plane(value):
    return moved(value, lambda p, z, y, c: (PIPE - 1 - p, z, y ^ c, c))


def to_owner(value):
    return moved(value, lambda p, z, y, c: (PIPE - 1 - p, z, c, y))


def to_far(value):
    return moved(value, lambda p, z, y, c: (p, z + 4, y, c))


def to_next(value):
    return moved(value, lambda p, z, y, c: (p + 1, z, y, c))


def to_z(value, k):
    return moved(value, lambda p, z, y, c: (p, z + k if c == 0 else z - k, y, c))


def place():
    dp = lax.axis_index("dp")
    return dp // 4, (dp // 2) % 2, dp % 2


def call(kernel, outs, args, specs=None, scratch=(), flops=0, after=()):
    specs = specs or [VM] * len(args)
    if after:
        used, body = len(args), kernel

        def kernel(*refs):
            body(*refs[:used], *refs[used + len(after) :])

    size = sum(a.size * a.dtype.itemsize for a in args) + sum(
        int(o.size) * o.dtype.itemsize for o in outs
    )
    return pl.pallas_call(
        kernel,
        out_shape=outs,
        in_specs=specs + [pl.BlockSpec(memory_space=pl.ANY)] * len(after),
        out_specs=[VM] * len(outs),
        scratch_shapes=list(scratch),
        compiler_params=pltpu.CompilerParams(vmem_limit_bytes=40 << 20),
        cost_estimate=pl.CostEstimate(flops=flops, bytes_accessed=size, transcendentals=0),
    )(*args, *after)


def shape(dims, dtype):
    return jax.ShapeDtypeStruct(dims, dtype)


def three_shifts(u):
    column = lax.broadcasted_iota(jnp.int32, u.shape, 0) % WD
    left = jnp.where(column == 0, 0.0, pltpu.roll(u, 1, 0))
    right = jnp.where(column == WD - 1, 0.0, pltpu.roll(u, PIX - 1, 0))
    return jnp.concatenate([left.astype(bf16), u.astype(bf16), right.astype(bf16)], axis=1)


def fill_padded(ref, value):
    edge = jnp.zeros((WD, value.shape[1]), value.dtype)
    ref[pl.ds(0, WD), :] = edge
    ref[pl.ds(WD, PIX), :] = value
    ref[pl.ds(WD + PIX, WD), :] = edge


def conv(col_ref, w_ref):
    total = None
    for a in range(3):
        part = jnp.dot(
            col_ref[pl.ds(a * WD, PIX), :],
            w_ref[pl.ds(3 * a, 3)].reshape(3 * C, C),
            preferred_element_type=f32,
        )
        total = part if total is None else total + part
    return total * SCALE


def conv_back(col_ref, w_ref):
    total = None
    for a in range(3):
        for b in range(3):
            part = lax.dot_general(
                col_ref[pl.ds((2 - a) * WD, PIX), pl.ds((2 - b) * C, C)],
                w_ref[3 * a + b],
                (((1,), (1,)), ((), ())),
                preferred_element_type=f32,
            )
            total = part if total is None else total + part
    return total * SCALE


def grads(xt_ref, dpad_ref, store):
    for a in range(3):
        g = jnp.dot(
            xt_ref[...], dpad_ref[pl.ds((2 - a) * WD, PIX), :], preferred_element_type=f32
        )
        for b in range(3):
            store(3 * a + b, (g[b * C : (b + 1) * C] * SCALE).reshape(Z * Y, 16, C))


def pair_kernel(own_ref, other_ref, far_ref, far_other_ref, pair_ref):
    _, _, core = place()
    for dz, mine, theirs in ((0, own_ref, other_ref), (1, far_ref, far_other_ref)):
        m, t = mine[...].astype(f32), theirs[...].astype(f32)
        low, high = jnp.where(core == 0, m, t), jnp.where(core == 0, t, m)
        pair_ref[dz] = jnp.concatenate([low, high], axis=1).astype(bf16)


def plane_kernel(split, first_ref, second_ref, chunk_ref, half_ref):
    _, y, core = place()
    half = y ^ core if split else y
    for dz in range(2):
        chunk_ref[dz, half] = first_ref[dz]
        chunk_ref[dz, 1 - half] = second_ref[dz]
        half_ref[dz] = chunk_ref[dz, core]


def assemble_kernel(chunk_ref, one_ref, one_core_ref, two_ref, two_core_ref, w_ref):
    z, _, core = place()
    sign = 2 * core - 1

    def put(source_z, source_y, value):
        w_ref[:, lax.rem(source_z + 2 * Z, Z) * 2 + source_y] = value

    for dz in range(2):
        for half in range(Y):
            put(z + 4 * dz, half, chunk_ref[dz, half])
            put(z + sign + 4 * dz, half, one_ref[dz, half])
            put(z - sign + 4 * dz, half, one_core_ref[dz, half])
        put(z + 2 * sign + 4 * dz, core, two_ref[dz])
        put(z - 2 * sign + 4 * dz, 1 - core, two_core_ref[dz])


def prep_kernel(u_ref, col_ref):
    fill_padded(col_ref, three_shifts(u_ref[...]))


def prep_stash_kernel(order_ref, stash_ref, col1_ref, xt1_ref, col2_ref, xt2_ref):
    for slot, col_ref, xt_ref in ((0, col1_ref, xt1_ref), (1, col2_ref, xt2_ref)):
        v3 = three_shifts(stash_ref[order_ref[0, slot]])
        fill_padded(col_ref, v3)
        xt_ref[...] = v3.T


def forward_first_kernel(col_ref, u_ref, w_ref, out_ref):
    pre = conv(col_ref, w_ref)
    out_ref[...] = (u_ref[...] + pre * jax.nn.sigmoid(pre)).astype(bf16)


def forward_second_kernel(arrived_ref, next_ref, w_ref, out_ref, col_ref):
    first = lax.axis_index("pipe") == 0
    u = jnp.where(first, next_ref[...], arrived_ref[...].astype(f32))
    fill_padded(col_ref, three_shifts(u))
    pre = conv(col_ref, w_ref)
    out_ref[...] = u + pre * jax.nn.sigmoid(pre)


def up_first_kernel(col_ref, g_ref, w_ref, back_ref, dpad_ref, dcol_ref):
    pre = conv(col_ref, w_ref)
    s = jax.nn.sigmoid(pre)
    g = g_ref[...]
    delta = (g * s * (1.0 + pre * (1.0 - s))).astype(bf16)
    fill_padded(dpad_ref, delta)
    fill_padded(dcol_ref, three_shifts(delta.astype(f32)))
    back_ref[...] = (g + conv_back(dcol_ref, w_ref)).astype(bf16)


def slope_kernel(col_ref, w_ref, slope_ref):
    pre = conv(col_ref, w_ref)
    s = jax.nn.sigmoid(pre)
    slope_ref[...] = s * (1.0 + pre * (1.0 - s))


def grad_first_kernel(xt_ref, dpad_ref, g_ref):
    def store(tap, value):
        g_ref[tap] = value

    grads(xt_ref, dpad_ref, store)


def share_out(total_ref, keep_ref, send_ref):
    z, _, core = place()
    sign = 1 - 2 * core

    def put(j, mine, theirs, mine_y, theirs_y):
        keep_ref[j] = total_ref[:, lax.rem(mine + 2 * Z, Z) * 2 + mine_y]
        send_ref[j] = total_ref[:, lax.rem(theirs + 2 * Z, Z) * 2 + theirs_y].astype(bf16)

    for dz in range(2):
        at = z + 4 * dz
        for half in range(Y):
            put(2 * dz + half, at + sign, at - sign, half, half)
        put(4 + dz, at + 2 * sign, at - 2 * sign, core, 1 - core)
        put(6 + dz, at, at, core, 1 - core)


def up_second_kernel(
    table_ref, index_ref, arrived_ref, next_ref, slope_ref, xt_ref, g_ref,
    keep_ref, send_ref, dpad_ref, cot_ref, total_ref,
):
    first = lax.axis_index("pipe") == 0
    factor = table_ref[index_ref[0]]
    cot = jnp.where(first, next_ref[...] * factor, arrived_ref[...].astype(f32))
    cot_ref[...] = cot
    fill_padded(dpad_ref, (cot * slope_ref[...]).astype(bf16))

    def store(tap, value):
        total_ref[tap] = g_ref[tap] + value

    grads(xt_ref, dpad_ref, store)
    share_out(total_ref, keep_ref, send_ref)


def up_out_kernel(cot_ref, dpad_ref, w_ref, out_ref, dcol_ref):
    delta = dpad_ref[pl.ds(WD, PIX), :].astype(f32)
    fill_padded(dcol_ref, three_shifts(delta))
    out_ref[...] = cot_ref[...] + conv_back(dcol_ref, w_ref)


def earlier_kernel(acc_ref, keep_ref, send_ref):
    share_out(acc_ref, keep_ref, send_ref)


def core_sum_kernel(keep_ref, got_ref, one_ref, two_ref, mine_ref):
    def total(j):
        return keep_ref[j] + got_ref[j].astype(f32)

    for dz in range(2):
        for half in range(Y):
            one_ref[dz, half] = total(2 * dz + half).astype(bf16)
        two_ref[dz] = total(4 + dz).astype(bf16)
        mine_ref[dz] = total(6 + dz)


def z_sum_kernel(one_ref, two_ref, mine_ref, keep_ref, send_ref):
    _, _, core = place()
    for dz in range(2):
        keep_ref[dz] = mine_ref[dz] + two_ref[dz].astype(f32) + one_ref[dz, core].astype(f32)
        send_ref[dz] = one_ref[dz, 1 - core]


def add_kernel(keep_ref, *refs):
    total = keep_ref[...]
    for ref in refs[:-1]:
        total = total + ref[...].astype(f32)
    refs[-1][...] = total.astype(bf16)


def last_split_kernel(got_ref, keep_ref, send_ref, total_ref):
    _, _, core = place()
    for dz in range(2):
        total_ref[...] = got_ref[dz].astype(f32).reshape(TAPS, CORES, 8, C)
        keep_ref[dz] = total_ref[:, core]
        send_ref[dz] = total_ref[:, 1 - core].astype(bf16)


def last_sum_kernel(keep_ref, got_ref, near_ref, far_ref):
    near_ref[...] = keep_ref[0] + got_ref[0].astype(f32)
    far_ref[...] = (keep_ref[1] + got_ref[1].astype(f32)).astype(bf16)


CONV_FLOPS = 2 * PIX * TAPS * C * C
COL = shape((PADDED, 3 * C), bf16)
DPAD = shape((PADDED, C), bf16)
FIELD = shape((PIX, C), f32)
FIELD16 = shape((PIX, C), bf16)
COL_SCRATCH = pltpu.VMEM((PADDED, 3 * C), bf16)
TOTAL = shape((TAPS, Z * Y, 16, C), f32)
CHUNK = shape((2, Y, TAPS, 16, C), bf16)
HALF = shape((2, TAPS, 16, C), bf16)
HALF32 = shape(HALF.shape, f32)


def assembled(chunk, half):
    one, two = to_z(chunk, 1), to_z(half, 2)
    args = [chunk, one, to_core(one), two, to_core(two)]
    w = call(assemble_kernel, [shape((TAPS, 16, 16, C), bf16)], args)[0]
    return w.reshape(TAPS, C, C)


def summed(keep, send):
    one, two, mine = call(core_sum_kernel, [CHUNK, HALF, HALF32], [keep, to_core(send)])
    got = [to_z(one, 1), to_z(two, 2)]
    keep, send = call(z_sum_kernel, [HALF32, HALF], got + [mine])
    return [keep, to_core(send)]


def body(
    master, grad_acc, down_act, down_next, up_stash, up_order, up_grad, up_next, ex_table, ex_index
):
    own = master.reshape(TAPS, 8, C).astype(bf16)
    far = to_far(own)
    pair = call(pair_kernel, [HALF], [own, to_core(own), far, to_core(far)])[0]

    got = to_plane(pair)
    chunk, half = call(functools.partial(plane_kernel, True), [CHUNK, HALF], [got, to_core(got)])
    w_mirror = assembled(chunk, half)

    own_other = to_y(pair)
    act = down_act.reshape(PIX, C)
    stash = up_stash.reshape(2, PIX, C)
    col1, xt1, col2, xt2 = call(
        prep_stash_kernel, [COL, shape((3 * C, PIX), bf16)] * 2, [up_order[0], stash], [SM, VM]
    )
    col_down = call(prep_kernel, [COL], [act])[0]

    lists = [shape((8, TAPS, 16, C), f32), shape((8, TAPS, 16, C), bf16)]
    keep_e, send_e = call(earlier_kernel, lists, [grad_acc.reshape(TAPS, Z * Y, 16, C)])
    earlier = summed(keep_e, send_e)
    earlier = call(add_kernel, [HALF], earlier)[0]
    earlier = to_mirror(earlier)

    back, dpad1 = call(
        up_first_kernel,
        [FIELD16, DPAD],
        [col1, up_grad.reshape(PIX, C), w_mirror],
        scratch=[COL_SCRATCH],
        flops=2 * CONV_FLOPS,
    )
    passed = to_next(back)
    own_chunk, own_half = call(
        functools.partial(plane_kernel, False), [CHUNK, HALF], [pair, own_other]
    )
    slope = call(slope_kernel, [FIELD], [col2, w_mirror], flops=CONV_FLOPS)[0]
    g1 = call(grad_first_kernel, [TOTAL], [xt1, dpad1], flops=CONV_FLOPS)[0]

    keep, send, dpad2, cot = call(
        up_second_kernel,
        lists + [DPAD, FIELD],
        [ex_table, ex_index, passed, up_next.reshape(PIX, C), slope, xt2, g1],
        [SM, SM, VM, VM, VM, VM, VM],
        scratch=[pltpu.VMEM((TAPS, Z * Y, 16, C), f32)],
        flops=CONV_FLOPS,
    )

    total = summed(keep, send)

    w_own = assembled(own_chunk, own_half)
    section_out = call(forward_first_kernel, [FIELD16], [col_down, act, w_own], flops=CONV_FLOPS)[0]
    arrived = to_next(section_out)
    up_out = call(
        up_out_kernel, [FIELD], [cot, dpad2, w_mirror], scratch=[COL_SCRATCH], flops=CONV_FLOPS
    )[0]
    down_out = call(
        forward_second_kernel,
        [FIELD],
        [arrived, down_next.reshape(PIX, C), w_own],
        scratch=[COL_SCRATCH],
        flops=CONV_FLOPS,
    )[0]

    total = call(add_kernel, [HALF], [*total, earlier])[0]
    parts = [shape((2, TAPS, 8, C), f32), shape((2, TAPS, 8, C), bf16)]
    keep_l, send_l = call(
        last_split_kernel, parts, [to_owner(total)], scratch=[pltpu.VMEM((TAPS, CORES, 8, C), f32)]
    )
    near_l, far_l = call(
        last_sum_kernel,
        [shape((TAPS, 8, C), f32), shape((TAPS, 8, C), bf16)],
        [keep_l, to_core(send_l)],
    )
    got_l = to_far(far_l)
    total_grad = near_l + got_l.astype(f32)
    new_master = master - learning_rate * total_grad.reshape(master.shape)
    field = (1, 1, HT, WD, C)
    return (down_out.reshape(field), up_out.reshape(field), new_master)


def solution(mesh):
    return jax.shard_map(
        body,
        mesh=mesh,
        in_specs=(
            P("pipe", None, None, "dp", None),
            P("dp", "pipe", None, None, None, None),
            P("pipe", "dp", None, None, None),
            P("dp", None, None, None),
            P("pipe", "dp", None, None, None, None),
            P("pipe", "dp", None),
            P("pipe", "dp", None, None, None),
            P("dp", None, None, None),
            P(),
            P("dp"),
        ),
        out_specs=(
            P("pipe", "dp", None, None, None),
            P("pipe", "dp", None, None, None),
            P("pipe", None, None, "dp", None),
        ),
        check_vma=False,
    )
```

```python
import functools

import jax
import jax.numpy as jnp
from jax import lax
from jax.experimental import pallas as pl
from jax.experimental.pallas import tpu as pltpu
from jax.sharding import PartitionSpec as P


learning_rate = 0.05
PIPE, Z, Y, CORES = 8, 8, 2, 2
C, HT, WD = 256, 16, 32
PIX = HT * WD
PADDED = PIX + 2 * WD
TAPS = 9
SCALE = (9.0 * C) ** (-0.5)
bf16, f32 = jnp.bfloat16, jnp.float32
VM = pl.BlockSpec(memory_space=pltpu.VMEM)
SM = pl.BlockSpec(memory_space=pltpu.SMEM)


def moved(value, where):
    pairs = []
    for p in range(PIPE):
        for z in range(Z):
            for y in range(Y):
                for c in range(CORES):
                    to = where(p, z, y, c)
                    if to is None:
                        continue
                    tp, tz, ty, tc = to
                    if not 0 <= tp < PIPE:
                        continue
                    target = tp * 32 + (tz % Z) * 4 + ty * 2 + tc
                    pairs.append((p * 32 + z * 4 + y * 2 + c, target))
    return lax.ppermute(value, ("pipe", "dp"), pairs)


def to_core(value):
    return moved(value, lambda p, z, y, c: (p, z, y, 1 - c))


def to_y(value):
    return moved(value, lambda p, z, y, c: (p, z, 1 - y, c))


def to_mirror(value):
    return moved(value, lambda p, z, y, c: (PIPE - 1 - p, z, y, c))


def to_mirror_y(value):
    return moved(value, lambda p, z, y, c: (PIPE - 1 - p, z, 1 - y, c))


def to_mirror_split(value):
    return moved(value, lambda p, z, y, c: (PIPE - 1 - p, z, y if c == 0 else 1 - y, c))


def to_next(value):
    return moved(value, lambda p, z, y, c: (p + 1, z, y, c))


def to_z(value, k):
    return moved(value, lambda p, z, y, c: (p, z + k if c == 0 else z - k, y, c))


def to_far(value):
    return moved(value, lambda p, z, y, c: (p, z + 4, y, c))


def place():
    dp = lax.axis_index("dp")
    return dp // 4, (dp // 2) % 2, dp % 2


def call(kernel, outs, args, specs=None, scratch=(), flops=0, after=()):
    specs = specs or [VM] * len(args)
    if after:
        used, body = len(args), kernel

        def kernel(*refs):
            body(*refs[:used], *refs[used + len(after) :])

    size = sum(a.size * a.dtype.itemsize for a in args) + sum(
        int(o.size) * o.dtype.itemsize for o in outs
    )
    return pl.pallas_call(
        kernel,
        out_shape=outs,
        in_specs=specs + [pl.BlockSpec(memory_space=pl.ANY)] * len(after),
        out_specs=[VM] * len(outs),
        scratch_shapes=list(scratch),
        compiler_params=pltpu.CompilerParams(vmem_limit_bytes=40 << 20),
        cost_estimate=pl.CostEstimate(flops=flops, bytes_accessed=size, transcendentals=0),
    )(*args, *after)


def shape(dims, dtype):
    return jax.ShapeDtypeStruct(dims, dtype)


def three_shifts(u):
    column = lax.broadcasted_iota(jnp.int32, u.shape, 0) % WD
    left = jnp.where(column == 0, 0.0, pltpu.roll(u, 1, 0))
    right = jnp.where(column == WD - 1, 0.0, pltpu.roll(u, PIX - 1, 0))
    return jnp.concatenate([left.astype(bf16), u.astype(bf16), right.astype(bf16)], axis=1)


def fill_padded(ref, value):
    edge = jnp.zeros((WD, value.shape[1]), value.dtype)
    ref[pl.ds(0, WD), :] = edge
    ref[pl.ds(WD, PIX), :] = value
    ref[pl.ds(WD + PIX, WD), :] = edge


def conv(col_ref, w_ref):
    total = None
    for a in range(3):
        part = jnp.dot(
            col_ref[pl.ds(a * WD, PIX), :],
            w_ref[pl.ds(3 * a, 3)].reshape(3 * C, C),
            preferred_element_type=f32,
        )
        total = part if total is None else total + part
    return total * SCALE


def conv_back(col_ref, w_ref):
    total = None
    for a in range(3):
        for b in range(3):
            part = lax.dot_general(
                col_ref[pl.ds((2 - a) * WD, PIX), pl.ds((2 - b) * C, C)],
                w_ref[3 * a + b],
                (((1,), (1,)), ((), ())),
                preferred_element_type=f32,
            )
            total = part if total is None else total + part
    return total * SCALE


def grads(xt_ref, dpad_ref, store):
    for a in range(3):
        g = jnp.dot(
            xt_ref[...], dpad_ref[pl.ds((2 - a) * WD, PIX), :], preferred_element_type=f32
        )
        for b in range(3):
            store(3 * a + b, (g[b * C : (b + 1) * C] * SCALE).reshape(Z * Y, 16, C))


def pair_kernel(own_ref, other_ref, pair_ref):
    _, _, core = place()
    mine, theirs = own_ref[...].astype(f32), other_ref[...].astype(f32)
    low, high = jnp.where(core == 0, mine, theirs), jnp.where(core == 0, theirs, mine)
    pair_ref[...] = jnp.concatenate([low, high], axis=1).astype(bf16)


def plane_kernel(split, first_ref, second_ref, chunk_ref, far_ref):
    _, y, core = place()
    half = y ^ core if split else y
    chunk_ref[half] = first_ref[...]
    chunk_ref[1 - half] = second_ref[...]
    far_ref[...] = chunk_ref[core]


def assemble_kernel(chunk_ref, *refs):
    w_ref = refs[-1]
    near, near_core = refs[0:3], refs[3:6]
    far_ref, far_core_ref = refs[6:8]
    z, _, core = place()

    def put(source_z, source_y, value):
        w_ref[:, lax.rem(source_z + 2 * Z, Z) * 2 + source_y] = value

    sign = 2 * core - 1
    for half in range(Y):
        put(z, half, chunk_ref[half])
        for k in range(3):
            put(z + sign * (k + 1), half, near[k][half])
            put(z - sign * (k + 1), half, near_core[k][half])
    put(z + 4, core, far_ref[...])
    put(z + 4, 1 - core, far_core_ref[...])


def prep_kernel(u_ref, col_ref):
    fill_padded(col_ref, three_shifts(u_ref[...]))


def prep_stash_kernel(order_ref, stash_ref, col1_ref, xt1_ref, col2_ref, xt2_ref):
    for slot, col_ref, xt_ref in ((0, col1_ref, xt1_ref), (1, col2_ref, xt2_ref)):
        v3 = three_shifts(stash_ref[order_ref[0, slot]])
        fill_padded(col_ref, v3)
        xt_ref[...] = v3.T


def forward_first_kernel(col_ref, u_ref, w_ref, out_ref):
    pre = conv(col_ref, w_ref)
    out_ref[...] = (u_ref[...] + pre * jax.nn.sigmoid(pre)).astype(bf16)


def forward_second_kernel(arrived_ref, next_ref, w_ref, out_ref, col_ref):
    first = lax.axis_index("pipe") == 0
    u = jnp.where(first, next_ref[...], arrived_ref[...].astype(f32))
    fill_padded(col_ref, three_shifts(u))
    pre = conv(col_ref, w_ref)
    out_ref[...] = u + pre * jax.nn.sigmoid(pre)


def up_first_kernel(col_ref, g_ref, w_ref, back_ref, dpad_ref, dcol_ref):
    pre = conv(col_ref, w_ref)
    s = jax.nn.sigmoid(pre)
    g = g_ref[...]
    delta = (g * s * (1.0 + pre * (1.0 - s))).astype(bf16)
    fill_padded(dpad_ref, delta)
    fill_padded(dcol_ref, three_shifts(delta.astype(f32)))
    back_ref[...] = (g + conv_back(dcol_ref, w_ref)).astype(bf16)


def slope_kernel(col_ref, w_ref, slope_ref):
    pre = conv(col_ref, w_ref)
    s = jax.nn.sigmoid(pre)
    slope_ref[...] = s * (1.0 + pre * (1.0 - s))


def grad_first_kernel(xt_ref, dpad_ref, g_ref):
    def store(tap, value):
        g_ref[tap] = value

    grads(xt_ref, dpad_ref, store)


def share_out(total_ref, keep_ref, send_ref):
    z, _, core = place()
    sign = 1 - 2 * core

    def spot(source_z, source_y):
        return lax.rem(source_z + 2 * Z, Z) * 2 + source_y

    for k in range(3):
        for half in range(Y):
            j = 2 * k + half
            keep_ref[j] = total_ref[:, spot(z + sign * (k + 1), half)]
            send_ref[j] = total_ref[:, spot(z - sign * (k + 1), half)].astype(bf16)
    for j, far in ((6, 4), (7, 0)):
        keep_ref[j] = total_ref[:, spot(z + far, core)]
        send_ref[j] = total_ref[:, spot(z + far, 1 - core)].astype(bf16)


def up_second_kernel(
    table_ref, index_ref, arrived_ref, next_ref, slope_ref, xt_ref, g_ref,
    keep_ref, send_ref, dpad_ref, cot_ref, total_ref,
):
    first = lax.axis_index("pipe") == 0
    factor = table_ref[index_ref[0]]
    cot = jnp.where(first, next_ref[...] * factor, arrived_ref[...].astype(f32))
    cot_ref[...] = cot
    fill_padded(dpad_ref, (cot * slope_ref[...]).astype(bf16))

    def store(tap, value):
        total_ref[tap] = g_ref[tap] + value

    grads(xt_ref, dpad_ref, store)
    share_out(total_ref, keep_ref, send_ref)


def up_out_kernel(cot_ref, dpad_ref, w_ref, out_ref, dcol_ref):
    delta = dpad_ref[pl.ds(WD, PIX), :].astype(f32)
    fill_padded(dcol_ref, three_shifts(delta))
    out_ref[...] = cot_ref[...] + conv_back(dcol_ref, w_ref)


def earlier_kernel(acc_ref, keep_ref, send_ref):
    share_out(acc_ref, keep_ref, send_ref)


def earlier_sum_kernel(keep_ref, got_ref, out_ref):
    out_ref[...] = (keep_ref[...] + got_ref[...].astype(f32)).astype(bf16)


def core_sum_kernel(keep_ref, got_ref, earlier_ref, m1_ref, m2_ref, m3_ref, m4_ref, mine_ref):
    def total(j):
        return keep_ref[j] + got_ref[j].astype(f32) + earlier_ref[j].astype(f32)

    for k, out_ref in enumerate((m1_ref, m2_ref, m3_ref)):
        for half in range(Y):
            out_ref[half] = total(2 * k + half).astype(bf16)
    m4_ref[...] = total(6).astype(bf16)
    mine_ref[...] = total(7)


def z_sum_kernel(m1_ref, m2_ref, m3_ref, m4_ref, mine_ref, keep_ref, send_ref, total_ref):
    _, _, core = place()
    for half in range(Y):
        total = m1_ref[half].astype(f32) + m2_ref[half].astype(f32) + m3_ref[half].astype(f32)
        total_ref[half] = total.reshape(TAPS, CORES, 8, C)
    last = m4_ref[...].astype(f32) + mine_ref[...]
    total_ref[core] += last.reshape(TAPS, CORES, 8, C)
    for half in range(Y):
        keep_ref[half] = total_ref[half, :, core]
        send_ref[half] = total_ref[half, :, 1 - core].astype(bf16)


def last_sum_kernel(keep_ref, got_ref, same_ref, other_ref):
    _, y, _ = place()
    for half, out_ref in ((y, same_ref), (1 - y, other_ref)):
        out_ref[...] = (keep_ref[half] + got_ref[half].astype(f32)).astype(bf16)


CONV_FLOPS = 2 * PIX * TAPS * C * C
COL = shape((PADDED, 3 * C), bf16)
DPAD = shape((PADDED, C), bf16)
FIELD = shape((PIX, C), f32)
FIELD16 = shape((PIX, C), bf16)
COL_SCRATCH = pltpu.VMEM((PADDED, 3 * C), bf16)
TOTAL = shape((TAPS, Z * Y, 16, C), f32)
CHUNK = shape((Y, TAPS, 16, C), bf16)
HALF = shape((TAPS, 16, C), bf16)


def gathered(chunk, far):
    near = [to_z(chunk, k) for k in (1, 2, 3)]
    near.append(to_far(far))
    return near, [to_core(n) for n in near]


def assembled(chunk, near, near_core):
    args = [chunk, *near[:3], *near_core[:3], near[3], near_core[3]]
    w = call(assemble_kernel, [shape((TAPS, 16, 16, C), bf16)], args)[0]
    return w.reshape(TAPS, C, C)


def body(
    master, grad_acc, down_act, down_next, up_stash, up_order, up_grad, up_next, ex_table, ex_index
):
    own = master.reshape(TAPS, 8, C).astype(bf16)
    pair = call(pair_kernel, [HALF], [own, to_core(own)])[0]

    mirror_pair = to_mirror_split(pair)
    mirror_chunk, mirror_far = call(
        functools.partial(plane_kernel, True), [CHUNK, HALF], [mirror_pair, to_core(mirror_pair)]
    )
    w_mirror = assembled(mirror_chunk, *gathered(mirror_chunk, mirror_far))

    own_other = to_y(pair)
    act = down_act.reshape(PIX, C)
    stash = up_stash.reshape(2, PIX, C)
    col1, xt1, col2, xt2 = call(
        prep_stash_kernel, [COL, shape((3 * C, PIX), bf16)] * 2, [up_order[0], stash], [SM, VM]
    )
    col_down = call(prep_kernel, [COL], [act])[0]

    lists = [shape((8, TAPS, 16, C), f32), shape((8, TAPS, 16, C), bf16)]
    keep_e, send_e = call(earlier_kernel, lists, [grad_acc.reshape(TAPS, Z * Y, 16, C)])
    earlier = call(earlier_sum_kernel, lists[1:], [keep_e, to_core(send_e)])[0]
    earlier_moved = to_mirror(earlier)

    back, dpad1 = call(
        up_first_kernel,
        [FIELD16, DPAD],
        [col1, up_grad.reshape(PIX, C), w_mirror],
        scratch=[COL_SCRATCH],
        flops=2 * CONV_FLOPS,
    )
    passed = to_next(back)
    own_chunk, own_far = call(
        functools.partial(plane_kernel, False), [CHUNK, HALF], [pair, own_other]
    )
    own_near, own_near_core = gathered(own_chunk, own_far)
    slope = call(slope_kernel, [FIELD], [col2, w_mirror], flops=CONV_FLOPS)[0]
    g1 = call(grad_first_kernel, [TOTAL], [xt1, dpad1], flops=CONV_FLOPS)[0]

    keep, send, dpad2, cot = call(
        up_second_kernel,
        lists + [DPAD, FIELD],
        [ex_table, ex_index, passed, up_next.reshape(PIX, C), slope, xt2, g1],
        [SM, SM, VM, VM, VM, VM, VM],
        scratch=[pltpu.VMEM((TAPS, Z * Y, 16, C), f32)],
        flops=CONV_FLOPS,
    )

    *messages, mine = call(
        core_sum_kernel,
        [CHUNK] * 3 + [HALF, shape((TAPS, 16, C), f32)],
        [keep, to_core(send), earlier_moved],
    )
    got = [to_z(messages[k - 1], k) for k in (1, 2, 3)]
    got.append(to_far(messages[3]))

    w_own = assembled(own_chunk, own_near, own_near_core)
    section_out = call(forward_first_kernel, [FIELD16], [col_down, act, w_own], flops=CONV_FLOPS)[0]
    arrived = to_next(section_out)
    up_out = call(
        up_out_kernel, [FIELD], [cot, dpad2, w_mirror], scratch=[COL_SCRATCH], flops=CONV_FLOPS
    )[0]
    down_out = call(
        forward_second_kernel,
        [FIELD],
        [arrived, down_next.reshape(PIX, C), w_own],
        scratch=[COL_SCRATCH],
        flops=CONV_FLOPS,
    )[0]

    parts = [shape((Y, TAPS, 8, C), f32), shape((Y, TAPS, 8, C), bf16)]
    keep_z, send_z = call(
        z_sum_kernel, parts, got + [mine], scratch=[pltpu.VMEM((Y, TAPS, CORES, 8, C), f32)]
    )
    same, other = call(last_sum_kernel, [shape((TAPS, 8, C), bf16)] * 2, [keep_z, to_core(send_z)])
    a, b = to_mirror(same), to_mirror_y(other)
    total_grad = a.astype(f32) + b.astype(f32)
    new_master = master - learning_rate * total_grad.reshape(master.shape)
    field = (1, 1, HT, WD, C)
    return (down_out.reshape(field), up_out.reshape(field), new_master)


def solution(mesh):
    return jax.shard_map(
        body,
        mesh=mesh,
        in_specs=(
            P("pipe", None, None, "dp", None),
            P("dp", "pipe", None, None, None, None),
            P("pipe", "dp", None, None, None),
            P("dp", None, None, None),
            P("pipe", "dp", None, None, None, None),
            P("pipe", "dp", None),
            P("pipe", "dp", None, None, None),
            P("dp", None, None, None),
            P(),
            P("dp"),
        ),
        out_specs=(
            P("pipe", "dp", None, None, None),
            P("pipe", "dp", None, None, None),
            P("pipe", None, None, "dp", None),
        ),
        check_vma=False,
    )
```
